768 devices in a mesh: batch: 8 (over y), dir: 96 (over z, x, core).
Axes of the slice: x: 4, y: 8, z: 12, core: 2. Of those that a mesh axis runs over, the one named last changes fastest.
Arguments:
- embeddings: bfloat16 [3072, 2048], P(('batch', 'dir')), may hold values from -13 to 13
- directions: bfloat16 [2048, 24576], P(None, 'dir'), may hold values from -0.125 to 0.125
Outputs:
- grad_embed: float32 [3072, 2048], P(('batch', 'dir'))
The draws below stay inside these ranges and needn't reach their ends.
All inputs are finite; a program needn't handle non-finite values.
Results may differ from the reference program's by a relative error of at most 0.0016.
Values may be sent and summed in bfloat16 or wider, within the bound.
No kernel may reach another device: no remote copies, remote signals or barrier semaphores. Data moves between devices by JAX's collectives and lax.ppermute only.
A program may use at most 32 MiB of HBM per device.

```python
import jax
import jax.numpy as jnp
from jax import lax

D = 2048
KNOTS = 17
DIR_DEV = 256
ROWS = 3072
DIRS = 24576
N_DIR = 96


def draw_embeddings(key, part):
    row_key = jax.random.fold_in(key, 11)
    value_key = jax.random.fold_in(key, 23)
    position = jnp.arange(ROWS, dtype=jnp.float32) / (ROWS - 1)
    jitter = jnp.clip(jax.random.normal(row_key, (ROWS,), jnp.float32), -3.0, 3.0)
    scale = 0.25 * jnp.power(10.0, position) * jnp.exp(0.3 * jitter)
    values = 0.35 * jnp.clip(jax.random.normal(value_key, (ROWS, D), jnp.float32), -5.0, 5.0) + 0.3
    return (values * scale[:, None]).astype(jnp.bfloat16)


def levels(stream_key, shape, cuts, low, top_value):
    def one(axis_at, shards_of):
        draws = jax.random.uniform(jax.random.fold_in(jax.random.fold_in(stream_key, 6), axis_at), (shards_of,), jnp.float32, low / len(cuts), top_value / len(cuts))
        return jnp.repeat(jnp.exp(draws), shape[axis_at] // shards_of).reshape((-1,) + (1,) * (len(shape) - axis_at - 1))

    level = one(*cuts[0])
    for cut in cuts[1:]:
        level = level * one(*cut)
    return level


def normal_values(key, shape, spread, reach, shards=(), held_as=jnp.bfloat16):
    result = jax.random.normal(key, shape, jnp.float32) * spread
    if len(shards) > 0:
        result = levels(key, shape, shards, -0.22, 0.18) * result
    return jnp.clip(result, min=-reach, max=reach).astype(held_as)


def setup_inputs(seed: int = 0) -> dict:
    key_list = jax.random.split(jax.random.key(seed), 3)
    return {
        "embeddings": draw_embeddings(jax.random.fold_in(key_list[2], 71), 0),
        "directions": normal_values(key_list[1], (D, DIRS), D ** -0.5, 0.125, ((1, 96),)),
    }


def knot_table():
    index = jnp.arange(KNOTS, dtype=jnp.float32)
    spacing = 3.0 / (KNOTS - 1)
    knot_pos = index * spacing
    target = jnp.exp(-0.5 * knot_pos * knot_pos)
    ends = jnp.where((index == 0) | (index == KNOTS - 1), 0.5, 1.0)
    weights = ends * spacing * target
    return (knot_pos, weights, target)

def reference(embeddings, directions):
    dir_float = directions.astype(jnp.float32)
    unit = (dir_float / jnp.sqrt(lax.optimization_barrier(jnp.sum(dir_float * dir_float, axis=0, keepdims=True)) + 1e-06)).astype(jnp.bfloat16)
    blocks = unit.reshape(D, N_DIR, DIR_DEV).transpose(1, 0, 2)
    knot_pos, weights, target = knot_table()

    def one_block(total, block):
        projected = jnp.dot(embeddings, block, preferred_element_type=jnp.float32)
        angles = knot_pos[:, None, None] * projected[None]
        cosine_vals = jnp.cos(angles)
        sine_vals = jnp.sin(angles)
        cos_mean = lax.optimization_barrier(jnp.sum(cosine_vals, axis=1)) / ROWS
        sin_mean = lax.optimization_barrier(jnp.sum(sine_vals, axis=1)) / ROWS
        cos_coef = 2.0 * weights[:, None] * (cos_mean - target[:, None])
        sin_coef = 2.0 * weights[:, None] * sin_mean
        grad_proj = lax.optimization_barrier(jnp.sum(knot_pos[:, None, None] * (cosine_vals * sin_coef[:, None, :] - sine_vals * cos_coef[:, None, :]), axis=0)).astype(jnp.bfloat16)
        return (total + jnp.dot(grad_proj, block.T, preferred_element_type=jnp.float32), None)
    start_total = jnp.zeros((embeddings.shape[0], D), jnp.float32)
    grad_embed, unused = lax.scan(one_block, start_total, blocks)
    return grad_embed
```

```python
import math

import jax
import jax.numpy as jnp
from jax import lax
from jax.experimental import pallas as pl
from jax.experimental.pallas import tpu as pltpu
from jax.sharding import Mesh, PartitionSpec as P

KNOTS = 17
STEP = 3.0 / (KNOTS - 1)
KNOT = [k * STEP for k in range(KNOTS)]
TARGET = [math.exp(-0.5 * t * t) for t in KNOT]
WEIGHT = [(0.5 if k in (0, KNOTS - 1) else 1.0) * STEP * TARGET[k] for k in range(KNOTS)]
TURN = (6.28125, 0.0019340515136719, 1.2556659146e-06)
TILE = 32
F32 = jnp.float32
BF16 = jnp.bfloat16


def base_angle(proj):
    theta = proj * STEP
    turns = jnp.round(theta * (0.5 / math.pi))
    q = 0.25 * (((theta - turns * TURN[0]) - turns * TURN[1]) - turns * TURN[2])
    z = q * q
    s = q * (1.0 + z * (-1.0 / 6 + z * (1.0 / 120 + z * (-1.0 / 5040 + z * (1.0 / 362880)))))
    c = 1.0 - z * (0.5 + z * (-1.0 / 24 + z * (1.0 / 720 + z * (-1.0 / 40320))))
    s2 = 2.0 * s * c
    c2 = 1.0 - 2.0 * s * s
    return 1.0 - 2.0 * s2 * s2, 2.0 * s2 * c2


def unit_kernel(dir_ref, unit_ref):
    width = dir_ref.shape[1]
    rows = 256
    total = jnp.zeros((8, width), F32)
    for i in range(dir_ref.shape[0] // rows):
        w = dir_ref[pl.ds(i * rows, rows), :].astype(F32)
        total = total + jnp.sum((w * w).reshape(rows // 8, 8, width), axis=0)
    inv = 1.0 / jnp.sqrt(jnp.sum(total, axis=0, keepdims=True) + 1e-06)
    for i in range(dir_ref.shape[0] // rows):
        w = dir_ref[pl.ds(i * rows, rows), :].astype(F32)
        unit_ref[pl.ds(i * rows, rows), :] = (w * inv).astype(BF16)


def sums_kernel(mine_ref, other_ref, unit_ref, c_ref, s_ref, out_ref, proj_ref, acc_ref):
    half = mine_ref.shape[0]
    rows, width = proj_ref.shape
    proj_ref[pl.ds(0, half), :] = jnp.dot(mine_ref[...], unit_ref[...], preferred_element_type=F32)
    proj_ref[pl.ds(half, half), :] = jnp.dot(other_ref[...], unit_ref[...], preferred_element_type=F32)
    acc_ref[...] = jnp.zeros_like(acc_ref)

    def fold(v):
        return jnp.sum(v.reshape(TILE // 8, 8, width), axis=0)

    @pl.loop(0, rows // TILE)
    def _(i):
        at = pl.ds(pl.multiple_of(i * TILE, TILE), TILE)
        c1, s1 = base_angle(proj_ref[at, :])
        c_ref[at, :] = c1
        s_ref[at, :] = s1
        two = c1 + c1
        acc_ref[0] += fold(c1)
        acc_ref[KNOTS - 1] += fold(s1)
        cp, sp, cc, sc = jnp.ones_like(c1), jnp.zeros_like(c1), c1, s1
        for k in range(1, KNOTS - 1):
            cp, cc = cc, two * cc - cp
            sp, sc = sc, two * sc - sp
            acc_ref[k] += fold(cc)
            acc_ref[KNOTS - 1 + k] += fold(sc)

    sums = jnp.sum(acc_ref[...], axis=1)
    for i in range(out_ref.shape[0]):
        out_ref[i] = sums


def grad_kernel(total_rows, c_ref, s_ref, sums_ref, unit_ref, mine_ref, out_ref, g_ref, rep_ref):
    rows, width = c_ref.shape
    half = rows // 2
    sums = jnp.sum(sums_ref[...], axis=0)
    for k in range(KNOTS):
        if k == 0:
            cos_total = jnp.full((1, width), total_rows, F32)
            sin_total = jnp.zeros((1, width), F32)
        else:
            cos_total = sums[k - 1 : k]
            sin_total = sums[KNOTS + k - 2 : KNOTS + k - 1]
        cos_coef = 2.0 * WEIGHT[k] * (cos_total / total_rows - TARGET[k])
        sin_coef = 2.0 * WEIGHT[k] * (sin_total / total_rows)
        rep_ref[k] = jnp.broadcast_to(KNOT[k] * sin_coef, (8, width))
        rep_ref[KNOTS + k] = jnp.broadcast_to(-KNOT[k] * cos_coef, (8, width))

    @pl.loop(0, rows // TILE)
    def _(i):
        at = pl.ds(pl.multiple_of(i * TILE, TILE), TILE)
        c1 = c_ref[at, :].reshape(TILE // 8, 8, width)
        s1 = s_ref[at, :].reshape(TILE // 8, 8, width)
        two = c1 + c1
        a2 = jnp.zeros_like(c1)
        b2 = a2
        a1 = rep_ref[KNOTS - 1] + a2
        b1 = rep_ref[2 * KNOTS - 1] + a2
        for k in range(KNOTS - 2, 0, -1):
            a1, a2 = rep_ref[k] + (two * a1 - a2), a1
            b1, b2 = rep_ref[KNOTS + k] + (two * b1 - b2), b1
        g = rep_ref[0] + (c1 * a1 - a2) + s1 * b1
        g_ref[at, :] = g.reshape(TILE, width).astype(BF16)

    mine_ref[...] = g_ref[pl.ds(0, half), :]
    times_unit(g_ref.at[pl.ds(half, half), :], unit_ref, out_ref)


def times_unit(g_ref, unit_ref, out_ref):
    step = 512
    for j in range(unit_ref.shape[0] // step):
        at = pl.ds(j * step, step)
        out_ref[:, at] = lax.dot_general(
            g_ref[...], unit_ref[at, :], (((1,), (1,)), ((), ())), preferred_element_type=F32
        )


def call(kernel, outs, scratch, flops, moved, operands):
    whole = pl.BlockSpec(memory_space=pltpu.VMEM)
    return pl.pallas_call(
        kernel,
        out_shape=outs,
        in_specs=[whole] * operands,
        out_specs=jax.tree.map(lambda _: whole, outs),
        scratch_shapes=scratch,
        compiler_params=pltpu.CompilerParams(vmem_limit_bytes=16 << 20),
        cost_estimate=pl.CostEstimate(flops=flops, bytes_accessed=moved, transcendentals=0),
    )


def to_all(x, axes, peers):
    return lax.all_to_all(jnp.broadcast_to(x[None], (peers,) + x.shape), axes, 0, 0, tiled=True)


def local(embeddings, directions):
    near, far, batch = lax.axis_size(("zl", "x")), lax.axis_size("zh"), lax.axis_size("y")
    swap = [(0, 1), (1, 0)]
    depth, width = directions.shape
    rows = embeddings.shape[0] * near * far
    total_rows = float(2 * rows * batch)
    sds = jax.ShapeDtypeStruct

    gathered = to_all(embeddings, "zh", far).reshape(-1, depth)
    mine = to_all(gathered, ("zl", "x"), near).reshape(rows, depth)
    other = lax.ppermute(mine, "c", swap)
    unit = call(unit_kernel, sds((depth, width), BF16), (), 4 * depth * width, 4 * depth * width, 1)(directions)

    c1, s1, sums = call(
        sums_kernel,
        (sds((2 * rows, width), F32), sds((2 * rows, width), F32), sds((batch, 2 * KNOTS - 2, width), F32)),
        (pltpu.VMEM((2 * rows, width), F32), pltpu.VMEM((2 * KNOTS - 2, 8, width), F32)),
        4 * rows * depth * width,
        8 * rows * depth,
        3,
    )(mine, other, unit)
    sums = lax.all_to_all(sums, "y", 0, 0, tiled=True)

    def grad(*refs):
        grad_kernel(total_rows, *refs)

    kept, theirs = call(
        grad,
        (sds((rows, width), BF16), sds((rows, depth), F32)),
        (pltpu.VMEM((2 * rows, width), BF16), pltpu.VMEM((2 * KNOTS, 8, width), F32)),
        2 * rows * depth * width,
        4 * rows * depth,
        4,
    )(c1, s1, sums, unit)
    arrived = lax.ppermute(theirs, "c", swap)
    ours = call(times_unit, sds((rows, depth), F32), (), 2 * rows * depth * width, 4 * rows * depth, 2)(kept, unit)
    part = (ours + arrived).astype(BF16).reshape(near, rows // near, depth)
    part = lax.all_to_all(part, ("zl", "x"), 0, 0, tiled=True)
    part = jnp.sum(part.astype(F32), axis=0).reshape(far, -1, depth)
    part = lax.all_to_all(part, "zh", 0, 0, tiled=True)
    return jnp.sum(part, axis=0)


def solution(mesh):
    fine = Mesh(mesh.devices.reshape(8, 4, 3, 4, 2), ("y", "zh", "zl", "x", "c"))
    along = ("zh", "zl", "x", "c")
    rows = P(("y",) + along, None)
    return jax.shard_map(local, mesh=fine, in_specs=(rows, P(None, along)), out_specs=rows, check_vma=False)
```

```python
import functools
import math

import jax
import jax.numpy as jnp
from jax import lax
from jax.experimental import pallas as pl
from jax.experimental.pallas import tpu as pltpu
from jax.sharding import Mesh, PartitionSpec as P

KNOTS = 17
STEP = 3.0 / (KNOTS - 1)
KNOT = [k * STEP for k in range(KNOTS)]
TARGET = [math.exp(-0.5 * t * t) for t in KNOT]
WEIGHT = [(0.5 if k in (0, KNOTS - 1) else 1.0) * STEP * TARGET[k] for k in range(KNOTS)]
TURN = (6.28125, 0.0019340515136719, 1.2556659146e-06)
TILE = 32
F32 = jnp.float32
BF16 = jnp.bfloat16
LINK = jnp.float16


def base_angle(proj):
    theta = proj * STEP
    turns = jnp.round(theta * (0.5 / math.pi))
    q = 0.25 * (((theta - turns * TURN[0]) - turns * TURN[1]) - turns * TURN[2])
    z = q * q
    s = q * (1.0 + z * (-1.0 / 6 + z * (1.0 / 120 + z * (-1.0 / 5040 + z * (1.0 / 362880)))))
    c = 1.0 - z * (0.5 + z * (-1.0 / 24 + z * (1.0 / 720 + z * (-1.0 / 40320))))
    s2 = 2.0 * s * c
    c2 = 1.0 - 2.0 * s * s
    return 1.0 - 2.0 * s2 * s2, 2.0 * s2 * c2


def unit_kernel(dir_ref, unit_ref):
    width = dir_ref.shape[1]
    rows = 256
    total = jnp.zeros((8, width), F32)
    for i in range(dir_ref.shape[0] // rows):
        w = dir_ref[pl.ds(i * rows, rows), :].astype(F32)
        total = total + jnp.sum((w * w).reshape(rows // 8, 8, width), axis=0)
    inv = 1.0 / jnp.sqrt(jnp.sum(total, axis=0, keepdims=True) + 1e-06)
    for i in range(dir_ref.shape[0] // rows):
        w = dir_ref[pl.ds(i * rows, rows), :].astype(F32)
        unit_ref[pl.ds(i * rows, rows), :] = (w * inv).astype(BF16)


def sums_kernel(local_rows, mine_ref, other_ref, unit_ref, c_ref, s_ref, out_ref, proj_ref, acc_ref):
    half = mine_ref.shape[0]
    rows, width = proj_ref.shape
    proj_ref[pl.ds(0, half), :] = jnp.dot(mine_ref[...], unit_ref[...], preferred_element_type=F32)
    proj_ref[pl.ds(half, half), :] = jnp.dot(other_ref[...], unit_ref[...], preferred_element_type=F32)
    acc_ref[...] = jnp.zeros_like(acc_ref)

    def fold(v):
        return jnp.sum(v.reshape(TILE // 8, 8, width), axis=0)

    @pl.loop(0, rows // TILE)
    def _(i):
        at = pl.ds(pl.multiple_of(i * TILE, TILE), TILE)
        c1, s1 = base_angle(proj_ref[at, :])
        c_ref[at, :] = c1
        s_ref[at, :] = s1
        two = c1 + c1
        acc_ref[0] += fold(c1)
        acc_ref[KNOTS - 1] += fold(s1)
        cp, sp, cc, sc = jnp.ones_like(c1), jnp.zeros_like(c1), c1, s1
        for k in range(1, KNOTS - 1):
            cp, cc = cc, two * cc - cp
            sp, sc = sc, two * sc - sp
            acc_ref[k] += fold(cc)
            acc_ref[KNOTS - 1 + k] += fold(sc)

    out_ref[...] = jnp.sum(acc_ref[...], axis=1)
    for k in range(1, KNOTS):
        out_ref[pl.ds(k - 1, 1), :] -= local_rows * TARGET[k]


def grad_kernel(total_rows, c_ref, s_ref, sums_ref, unit_ref, mine_ref, out_ref, g_ref, rep_ref):
    rows, width = c_ref.shape
    half = rows // 2
    sums = jnp.sum(sums_ref[...], axis=0)
    for k in range(KNOTS):
        if k == 0:
            cos_off = jnp.full((1, width), total_rows * (1.0 - TARGET[0]), F32)
            sin_total = jnp.zeros((1, width), F32)
        else:
            cos_off = sums[k - 1 : k]
            sin_total = sums[KNOTS + k - 2 : KNOTS + k - 1]
        cos_coef = 2.0 * WEIGHT[k] * (cos_off / total_rows)
        sin_coef = 2.0 * WEIGHT[k] * (sin_total / total_rows)
        rep_ref[k] = jnp.broadcast_to(KNOT[k] * sin_coef, (8, width))
        rep_ref[KNOTS + k] = jnp.broadcast_to(-KNOT[k] * cos_coef, (8, width))

    @pl.loop(0, rows // TILE)
    def _(i):
        at = pl.ds(pl.multiple_of(i * TILE, TILE), TILE)
        c1 = c_ref[at, :].reshape(TILE // 8, 8, width)
        s1 = s_ref[at, :].reshape(TILE // 8, 8, width)
        two = c1 + c1
        a2 = jnp.zeros_like(c1)
        b2 = a2
        a1 = rep_ref[KNOTS - 1] + a2
        b1 = rep_ref[2 * KNOTS - 1] + a2
        for k in range(KNOTS - 2, 0, -1):
            a1, a2 = rep_ref[k] + (two * a1 - a2), a1
            b1, b2 = rep_ref[KNOTS + k] + (two * b1 - b2), b1
        g = rep_ref[0] + (c1 * a1 - a2) + s1 * b1
        g_ref[at, :] = g.reshape(TILE, width).astype(BF16)

    mine_ref[...] = g_ref[pl.ds(0, half), :]
    times_unit(g_ref.at[pl.ds(half, half), :], unit_ref, out_ref)


def times_unit(g_ref, unit_ref, out_ref):
    step = 512
    for j in range(unit_ref.shape[0] // step):
        at = pl.ds(j * step, step)
        out_ref[:, at] = lax.dot_general(
            g_ref[...], unit_ref[at, :], (((1,), (1,)), ((), ())), preferred_element_type=F32
        )


def call(kernel, outs, scratch, flops, moved, operands):
    whole = pl.BlockSpec(memory_space=pltpu.VMEM)
    return pl.pallas_call(
        kernel,
        out_shape=outs,
        in_specs=[whole] * operands,
        out_specs=jax.tree.map(lambda _: whole, outs),
        scratch_shapes=scratch,
        compiler_params=pltpu.CompilerParams(vmem_limit_bytes=16 << 20),
        cost_estimate=pl.CostEstimate(flops=flops, bytes_accessed=moved, transcendentals=0),
    )


def to_all(x, axes, peers):
    return lax.all_to_all(jnp.broadcast_to(x[None], (peers,) + x.shape), axes, 0, 0, tiled=True)


def turn(x, axis, by):
    n = lax.axis_size(axis)
    return lax.ppermute(x, axis, [(i, (i + by) % n) for i in range(n)])


def local(embeddings, directions):
    ring, along_x, batch = lax.axis_size("z"), lax.axis_size("x"), lax.axis_size("y")
    depth, width = directions.shape
    block = embeddings.shape[0] * ring
    rows = block * along_x
    total_rows = float(2 * rows * batch)
    sds = jax.ShapeDtypeStruct

    held = to_all(embeddings, "z", ring).reshape(block, depth)
    far = [turn(held, "x", by) for by in (2, 1, along_x - 1)]
    mine = jnp.concatenate([held] + far, axis=0)
    other = turn(mine, "c", 1)
    unit = call(unit_kernel, sds((depth, width), BF16), (), 4 * depth * width, 4 * depth * width, 1)(directions)

    c1, s1, sums = call(
        functools.partial(sums_kernel, 2.0 * rows),
        (sds((2 * rows, width), F32), sds((2 * rows, width), F32), sds((2 * KNOTS - 2, width), F32)),
        (pltpu.VMEM((2 * rows, width), F32), pltpu.VMEM((2 * KNOTS - 2, 8, width), F32)),
        4 * rows * depth * width,
        8 * rows * depth,
        3,
    )(mine, other, unit)
    sums = to_all(sums.astype(LINK), "y", batch).astype(F32)

    kept, theirs = call(
        functools.partial(grad_kernel, total_rows),
        (sds((rows, width), BF16), sds((rows, depth), F32)),
        (pltpu.VMEM((2 * rows, width), BF16), pltpu.VMEM((2 * KNOTS, 8, width), F32)),
        2 * rows * depth * width,
        4 * rows * depth,
        4,
    )(c1, s1, sums, unit)
    arrived = turn(theirs, "c", 1)
    ours = call(times_unit, sds((rows, depth), F32), (), 2 * rows * depth * width, 4 * rows * depth, 2)(kept, unit)
    parts = (ours + arrived).reshape(along_x, block, depth)
    back = [turn(parts[j].astype(LINK), "x", by) for j, by in ((1, 2), (2, along_x - 1), (3, 1))]
    part = parts[0] + sum(p.astype(F32) for p in back)
    part = part.astype(LINK).reshape(ring, -1, depth)
    part = lax.all_to_all(part, "z", 0, 0, tiled=True)
    return jnp.sum(part.astype(F32), axis=0)


def solution(mesh):
    fine = Mesh(mesh.devices.reshape(8, 12, 4, 2), ("y", "z", "x", "c"))
    along = ("z", "x", "c")
    rows = P(("y",) + along, None)
    return jax.shard_map(local, mesh=fine, in_specs=(rows, P(None, along)), out_specs=rows, check_vma=False)
```

```python
import functools
import math

import jax
import jax.numpy as jnp
from jax import lax
from jax.experimental import pallas as pl
from jax.experimental.pallas import tpu as pltpu
from jax.sharding import Mesh, PartitionSpec as P

KNOTS = 17
STEP = 3.0 / (KNOTS - 1)
KNOT = [k * STEP for k in range(KNOTS)]
TARGET = [math.exp(-0.5 * t * t) for t in KNOT]
WEIGHT = [(0.5 if k in (0, KNOTS - 1) else 1.0) * STEP * TARGET[k] for k in range(KNOTS)]
TURN = (6.28125, 0.0019340515136719, 1.2556659146e-06)
TILE = 32
F32 = jnp.float32
BF16 = jnp.bfloat16
LINK = jnp.float16


def base_angle(proj):
    theta = proj * STEP
    turns = jnp.round(theta * (0.5 / math.pi))
    q = 0.25 * (((theta - turns * TURN[0]) - turns * TURN[1]) - turns * TURN[2])
    z = q * q
    s = q * (1.0 + z * (-1.0 / 6 + z * (1.0 / 120 + z * (-1.0 / 5040 + z * (1.0 / 362880)))))
    c = 1.0 - z * (0.5 + z * (-1.0 / 24 + z * (1.0 / 720 + z * (-1.0 / 40320))))
    s2 = 2.0 * s * c
    c2 = 1.0 - 2.0 * s * s
    return 1.0 - 2.0 * s2 * s2, 2.0 * s2 * c2


def unit_kernel(dir_ref, unit_ref):
    width = dir_ref.shape[1]
    rows = 256
    total = jnp.zeros((8, width), F32)
    for i in range(dir_ref.shape[0] // rows):
        w = dir_ref[pl.ds(i * rows, rows), :].astype(F32)
        total = total + jnp.sum((w * w).reshape(rows // 8, 8, width), axis=0)
    inv = 1.0 / jnp.sqrt(jnp.sum(total, axis=0, keepdims=True) + 1e-06)
    for i in range(dir_ref.shape[0] // rows):
        w = dir_ref[pl.ds(i * rows, rows), :].astype(F32)
        unit_ref[pl.ds(i * rows, rows), :] = (w * inv).astype(BF16)


def sums_kernel(rows_ref, unit_ref, more_ref, c_ref, s_ref, out_ref, proj_ref, acc_ref):
    rows, width = proj_ref.shape
    half = width // 2
    proj_ref[:, pl.ds(0, half)] = jnp.dot(rows_ref[...], unit_ref[...], preferred_element_type=F32)
    proj_ref[:, pl.ds(half, half)] = jnp.dot(rows_ref[...], more_ref[...], preferred_element_type=F32)
    acc_ref[...] = jnp.zeros_like(acc_ref)

    def fold(v):
        return jnp.sum(v.reshape(TILE // 8, 8, width), axis=0)

    @pl.loop(0, rows // TILE)
    def _(i):
        at = pl.ds(pl.multiple_of(i * TILE, TILE), TILE)
        c1, s1 = base_angle(proj_ref[at, :])
        c_ref[at, :] = c1
        s_ref[at, :] = s1
        two = c1 + c1
        acc_ref[0] += fold(c1)
        acc_ref[KNOTS - 1] += fold(s1)
        cp, sp, cc, sc = jnp.ones_like(c1), jnp.zeros_like(c1), c1, s1
        for k in range(1, KNOTS - 1):
            cp, cc = cc, two * cc - cp
            sp, sc = sc, two * sc - sp
            acc_ref[k] += fold(cc)
            acc_ref[KNOTS - 1 + k] += fold(sc)

    out_ref[...] = jnp.sum(acc_ref[...], axis=1)
    for k in range(1, KNOTS):
        out_ref[pl.ds(k - 1, 1), :] -= rows * TARGET[k]


def grad_kernel(total_rows, c_ref, s_ref, sums_ref, unit_ref, more_ref, out_ref, g_ref, rep_ref):
    rows, width = c_ref.shape
    sums = jnp.sum(sums_ref[...], axis=0)
    for k in range(KNOTS):
        if k == 0:
            cos_off = jnp.full((1, width), total_rows * (1.0 - TARGET[0]), F32)
            sin_total = jnp.zeros((1, width), F32)
        else:
            cos_off = sums[k - 1 : k]
            sin_total = sums[KNOTS + k - 2 : KNOTS + k - 1]
        cos_coef = 2.0 * WEIGHT[k] * (cos_off / total_rows)
        sin_coef = 2.0 * WEIGHT[k] * (sin_total / total_rows)
        rep_ref[k] = jnp.broadcast_to(KNOT[k] * sin_coef, (8, width))
        rep_ref[KNOTS + k] = jnp.broadcast_to(-KNOT[k] * cos_coef, (8, width))

    @pl.loop(0, rows // TILE)
    def _(i):
        at = pl.ds(pl.multiple_of(i * TILE, TILE), TILE)
        c1 = c_ref[at, :].reshape(TILE // 8, 8, width)
        s1 = s_ref[at, :].reshape(TILE // 8, 8, width)
        two = c1 + c1
        a2 = jnp.zeros_like(c1)
        b2 = a2
        a1 = rep_ref[KNOTS - 1] + a2
        b1 = rep_ref[2 * KNOTS - 1] + a2
        for k in range(KNOTS - 2, 0, -1):
            a1, a2 = rep_ref[k] + (two * a1 - a2), a1
            b1, b2 = rep_ref[KNOTS + k] + (two * b1 - b2), b1
        g = rep_ref[0] + (c1 * a1 - a2) + s1 * b1
        g_ref[at, :] = g.reshape(TILE, width).astype(BF16)

    step, half = 512, width // 2
    for j in range(unit_ref.shape[0] // step):
        at = pl.ds(j * step, step)
        out_ref[:, at] = times_transposed(g_ref[:, pl.ds(0, half)], unit_ref[at, :]) + times_transposed(
            g_ref[:, pl.ds(half, half)], more_ref[at, :]
        )


def times_transposed(a, b):
    return lax.dot_general(a, b, (((1,), (1,)), ((), ())), preferred_element_type=F32)


def call(kernel, outs, scratch, flops, moved, operands):
    whole = pl.BlockSpec(memory_space=pltpu.VMEM)
    return pl.pallas_call(
        kernel,
        out_shape=outs,
        in_specs=[whole] * operands,
        out_specs=jax.tree.map(lambda _: whole, outs),
        scratch_shapes=scratch,
        compiler_params=pltpu.CompilerParams(vmem_limit_bytes=16 << 20),
        cost_estimate=pl.CostEstimate(flops=flops, bytes_accessed=moved, transcendentals=0),
    )


def to_all(x, axes, peers):
    return lax.all_to_all(jnp.broadcast_to(x[None], (peers,) + x.shape), axes, 0, 0, tiled=True)


def turn(x, axis, by):
    n = lax.axis_size(axis)
    return lax.ppermute(x, axis, [(i, (i + by) % n) for i in range(n)])


def local(embeddings, directions):
    ring, along_x, batch = lax.axis_size("z"), lax.axis_size("x"), lax.axis_size("y")
    depth, width = directions.shape
    block = embeddings.shape[0] * ring
    rows = block * along_x
    total_rows = float(2 * rows * batch)
    sds = jax.ShapeDtypeStruct

    held = to_all(embeddings, "z", ring).reshape(block, depth)
    far = [turn(held, "x", by) for by in (2, 1, along_x - 1)]
    directions, anchor = lax.optimization_barrier((directions, held))
    units = [
        call(unit_kernel, sds((depth, width), BF16), (), 4 * depth * width, 4 * depth * width, 1)(d)
        for d in (directions, turn(directions, "c", 1))
    ]
    mine = jnp.concatenate([anchor] + far, axis=0)

    c1, s1, sums = call(
        sums_kernel,
        (sds((rows, 2 * width), F32), sds((rows, 2 * width), F32), sds((2 * KNOTS - 2, 2 * width), F32)),
        (pltpu.VMEM((rows, 2 * width), F32), pltpu.VMEM((2 * KNOTS - 2, 8, 2 * width), F32)),
        4 * rows * depth * width,
        8 * rows * depth,
        3,
    )(mine, *units)
    swapped = turn(sums, "c", 1)
    sums = sums + jnp.concatenate([swapped[:, width:], swapped[:, :width]], axis=1)
    sums = to_all(sums.astype(LINK), "y", batch).astype(F32)

    parts = call(
        functools.partial(grad_kernel, total_rows),
        sds((rows, depth), F32),
        (pltpu.VMEM((rows, 2 * width), BF16), pltpu.VMEM((2 * KNOTS, 8, 2 * width), F32)),
        4 * rows * depth * width,
        4 * rows * depth,
        5,
    )(c1, s1, sums, *units).reshape(along_x, block, depth)
    back = [turn(parts[j].astype(LINK), "x", by) for j, by in ((1, 2), (2, along_x - 1), (3, 1))]
    part = parts[0] + sum(p.astype(F32) for p in back)
    part = part.astype(LINK).reshape(ring, -1, depth)
    part = lax.all_to_all(part, "z", 0, 0, tiled=True)
    return jnp.sum(part.astype(F32), axis=0)


def solution(mesh):
    fine = Mesh(mesh.devices.reshape(8, 12, 4, 2), ("y", "z", "x", "c"))
    along = ("z", "x", "c")
    rows = P(("y",) + along, None)
    return jax.shard_map(local, mesh=fine, in_specs=(rows, P(None, along)), out_specs=rows, check_vma=False)
```

```python
import functools
import math

import jax
import jax.numpy as jnp
from jax import lax
from jax.experimental import pallas as pl
from jax.experimental.pallas import tpu as pltpu
from jax.sharding import Mesh, PartitionSpec as P


KNOTS = 17
STEP = 3.0 / (KNOTS - 1)
KNOT = [k * STEP for k in range(KNOTS)]
TARGET = [math.exp(-0.5 * t * t) for t in KNOT]
WEIGHT = [(0.5 if k in (0, KNOTS - 1) else 1.0) * STEP * TARGET[k] for k in range(KNOTS)]
TURN = (6.28125, 0.0019340515136719, 1.2556659146e-06)
TILE = 16
F32 = jnp.float32
BF16 = jnp.bfloat16
LINK = jnp.float16


def base_angle(proj):
    theta = proj * STEP
    turns = jnp.round(theta * (0.5 / math.pi))
    q = 0.25 * (((theta - turns * TURN[0]) - turns * TURN[1]) - turns * TURN[2])
    z = q * q
    s = q * (1.0 + z * (-1.0 / 6 + z * (1.0 / 120 + z * (-1.0 / 5040 + z * (1.0 / 362880)))))
    c = 1.0 - z * (0.5 + z * (-1.0 / 24 + z * (1.0 / 720 + z * (-1.0 / 40320))))
    s2 = 2.0 * s * c
    c2 = 1.0 - 2.0 * s * s
    return 1.0 - 2.0 * s2 * s2, 2.0 * s2 * c2


def unit_kernel(dir_ref, unit_ref):
    width = dir_ref.shape[1]
    rows = 256
    total = jnp.zeros((8, width), F32)
    for i in range(dir_ref.shape[0] // rows):
        w = dir_ref[pl.ds(i * rows, rows), :].astype(F32)
        total = total + jnp.sum((w * w).reshape(rows // 8, 8, width), axis=0)
    inv = 1.0 / jnp.sqrt(jnp.sum(total, axis=0, keepdims=True) + 1e-06)
    for i in range(dir_ref.shape[0] // rows):
        w = dir_ref[pl.ds(i * rows, rows), :].astype(F32)
        unit_ref[pl.ds(i * rows, rows), :] = (w * inv).astype(BF16)


def sums_kernel(first, rows_ref, unit_ref, more_ref, *refs):
    c_ref, s_ref, out_ref, proj_ref, acc_ref = refs if first else refs[1:]
    rows, width = proj_ref.shape
    half = width // 2
    proj_ref[:, pl.ds(0, half)] = jnp.dot(rows_ref[...], unit_ref[...], preferred_element_type=F32)
    proj_ref[:, pl.ds(half, half)] = jnp.dot(rows_ref[...], more_ref[...], preferred_element_type=F32)
    acc_ref[...] = jnp.zeros_like(acc_ref)

    def fold(v):
        return jnp.sum(v.reshape(TILE // 8, 8, width), axis=0)

    @pl.loop(0, rows // TILE)
    def _(i):
        at = pl.ds(pl.multiple_of(i * TILE, TILE), TILE)
        c1, s1 = base_angle(proj_ref[at, :])
        c_ref[at, :] = c1
        s_ref[at, :] = s1
        two = c1 + c1
        acc_ref[0] += fold(c1)
        acc_ref[KNOTS - 1] += fold(s1)
        cp, sp, cc, sc = jnp.ones_like(c1), jnp.zeros_like(c1), c1, s1
        for k in range(1, KNOTS - 1):
            cp, cc = cc, two * cc - cp
            sp, sc = sc, two * sc - sp
            acc_ref[k] += fold(cc)
            acc_ref[KNOTS - 1 + k] += fold(sc)

    sums = jnp.sum(acc_ref[...], axis=1)
    out_ref[...] = sums if first else sums + refs[0][...]
    for k in range(1, KNOTS):
        out_ref[pl.ds(k - 1, 1), :] -= rows * TARGET[k]


def grad_kernel(total_rows, c_ref, s_ref, sums_ref, unit_ref, more_ref, out_ref, g_ref, rep_ref):
    rows, width = c_ref.shape
    sums = jnp.sum(sums_ref[...], axis=0)
    for k in range(KNOTS):
        if k == 0:
            cos_off = jnp.full((1, width), total_rows * (1.0 - TARGET[0]), F32)
            sin_total = jnp.zeros((1, width), F32)
        else:
            cos_off = sums[k - 1 : k]
            sin_total = sums[KNOTS + k - 2 : KNOTS + k - 1]
        cos_coef = 2.0 * WEIGHT[k] * (cos_off / total_rows)
        sin_coef = 2.0 * WEIGHT[k] * (sin_total / total_rows)
        rep_ref[k] = jnp.broadcast_to(KNOT[k] * sin_coef, (8, width))
        rep_ref[KNOTS + k] = jnp.broadcast_to(-KNOT[k] * cos_coef, (8, width))

    @pl.loop(0, rows // TILE)
    def _(i):
        at = pl.ds(pl.multiple_of(i * TILE, TILE), TILE)
        c1 = c_ref[at, :].reshape(TILE // 8, 8, width)
        s1 = s_ref[at, :].reshape(TILE // 8, 8, width)
        two = c1 + c1
        a2 = jnp.zeros_like(c1)
        b2 = a2
        a1 = rep_ref[KNOTS - 1] + a2
        b1 = rep_ref[2 * KNOTS - 1] + a2
        for k in range(KNOTS - 2, 0, -1):
            a1, a2 = rep_ref[k] + (two * a1 - a2), a1
            b1, b2 = rep_ref[KNOTS + k] + (two * b1 - b2), b1
        g = rep_ref[0] + (c1 * a1 - a2) + s1 * b1
        g_ref[at, :] = g.reshape(TILE, width).astype(BF16)

    step, half = 512, width // 2
    for j in range(unit_ref.shape[0] // step):
        at = pl.ds(j * step, step)
        out_ref[:, at] = times_transposed(g_ref[:, pl.ds(0, half)], unit_ref[at, :]) + times_transposed(
            g_ref[:, pl.ds(half, half)], more_ref[at, :]
        )


def times_transposed(a, b):
    return lax.dot_general(a, b, (((1,), (1,)), ((), ())), preferred_element_type=F32)


def call(kernel, outs, scratch, flops, moved, operands):
    whole = pl.BlockSpec(memory_space=pltpu.VMEM)
    return pl.pallas_call(
        kernel,
        out_shape=outs,
        in_specs=[whole] * operands,
        out_specs=jax.tree.map(lambda _: whole, outs),
        scratch_shapes=scratch,
        compiler_params=pltpu.CompilerParams(vmem_limit_bytes=16 << 20),
        cost_estimate=pl.CostEstimate(flops=flops, bytes_accessed=moved, transcendentals=0),
    )


def to_all(x, axes, peers):
    return lax.all_to_all(jnp.broadcast_to(x[None], (peers,) + x.shape), axes, 0, 0, tiled=True)


def turn(x, axis, by):
    n = lax.axis_size(axis)
    return lax.ppermute(x, axis, [(i, (i + by) % n) for i in range(n)])


def local(embeddings, directions):
    ring, along_x, batch = lax.axis_size("z"), lax.axis_size("x"), lax.axis_size("y")
    depth, width = directions.shape
    block = embeddings.shape[0] * ring
    total_rows = float(2 * block * along_x * batch)
    sds = jax.ShapeDtypeStruct

    held = to_all(embeddings, "z", ring).reshape(block, depth)
    order = (2, 1, along_x - 1)
    rows = {0: held}
    for by in order:
        rows[by] = turn(held, "x", by)
    sent, rows[0] = lax.optimization_barrier((directions, held))
    theirs = turn(sent, "c", 1)
    units = []
    for columns in (directions, theirs):
        units.append(call(unit_kernel, sds((depth, width), BF16), (), 4 * depth * width, 4 * depth * width, 1)(columns))

    waves, sums = {}, ()
    for by in (0,) + order:
        c1, s1, total = call(
            functools.partial(sums_kernel, not sums),
            (sds((block, 2 * width), F32), sds((block, 2 * width), F32), sds((2 * KNOTS - 2, 2 * width), F32)),
            (pltpu.VMEM((block, 2 * width), F32), pltpu.VMEM((2 * KNOTS - 2, 8, 2 * width), F32)),
            4 * block * depth * width,
            8 * block * depth,
            3 + len(sums),
        )(rows[by], *units, *sums)
        waves[by], sums = (c1, s1), (total,)
    (sums,) = sums
    swapped = turn(sums, "c", 1)
    sums = sums + jnp.concatenate([swapped[:, width:], swapped[:, :width]], axis=1)
    sums = to_all(sums.astype(LINK), "y", batch).astype(F32)

    parts = {}
    for by in (2, along_x - 1, 1, 0):
        parts[by] = call(
            functools.partial(grad_kernel, total_rows),
            sds((block, depth), F32),
            (pltpu.VMEM((block, 2 * width), BF16), pltpu.VMEM((2 * KNOTS, 8, 2 * width), F32)),
            4 * block * depth * width,
            4 * block * depth,
            5,
        )(*waves[by], sums, *units)
        if by:
            parts[by] = turn(parts[by].astype(LINK), "x", along_x - by)
    part = sum(parts[by].astype(F32) for by in (0,) + order)
    part = part.astype(LINK).reshape(ring, -1, depth)
    part = lax.all_to_all(part, "z", 0, 0, tiled=True)
    return jnp.sum(part.astype(F32), axis=0)


def solution(mesh):
    fine = Mesh(mesh.devices.reshape(8, 12, 4, 2), ("y", "z", "x", "c"))
    along = ("z", "x", "c")
    rows = P(("y",) + along, None)

    return jax.shard_map(local, mesh=fine, in_specs=(rows, P(None, along)), out_specs=rows, check_vma=False)
```

```python
import functools
import math

import jax
import jax.numpy as jnp
from jax import lax
from jax.experimental import pallas as pl
from jax.experimental.pallas import tpu as pltpu
from jax.sharding import Mesh, PartitionSpec as P


KNOTS = 17
STEP = 3.0 / (KNOTS - 1)
KNOT = [k * STEP for k in range(KNOTS)]
TARGET = [math.exp(-0.5 * t * t) for t in KNOT]
WEIGHT = [(0.5 if k in (0, KNOTS - 1) else 1.0) * STEP * TARGET[k] for k in range(KNOTS)]
TURN = (6.28125, 0.0019340515136719, 1.2556659146e-06)
TILE = 16
F32 = jnp.float32
BF16 = jnp.bfloat16
LINK = jnp.float16


def base_angle(proj):
    theta = proj * STEP
    turns = jnp.round(theta * (0.5 / math.pi))
    q = 0.25 * (((theta - turns * TURN[0]) - turns * TURN[1]) - turns * TURN[2])
    z = q * q
    s = q * (1.0 + z * (-1.0 / 6 + z * (1.0 / 120 + z * (-1.0 / 5040 + z * (1.0 / 362880)))))
    c = 1.0 - z * (0.5 + z * (-1.0 / 24 + z * (1.0 / 720 + z * (-1.0 / 40320))))
    s2 = 2.0 * s * c
    c2 = 1.0 - 2.0 * s * s
    return 1.0 - 2.0 * s2 * s2, 2.0 * s2 * c2


def unit_kernel(dir_ref, unit_ref):
    width = dir_ref.shape[1]
    rows = 256
    total = jnp.zeros((8, width), F32)
    for i in range(dir_ref.shape[0] // rows):
        w = dir_ref[pl.ds(i * rows, rows), :].astype(F32)
        total = total + jnp.sum((w * w).reshape(rows // 8, 8, width), axis=0)
    inv = 1.0 / jnp.sqrt(jnp.sum(total, axis=0, keepdims=True) + 1e-06)
    for i in range(dir_ref.shape[0] // rows):
        w = dir_ref[pl.ds(i * rows, rows), :].astype(F32)
        unit_ref[pl.ds(i * rows, rows), :] = (w * inv).astype(BF16)


def sums_kernel(rows_ref, unit_ref, more_ref, c_ref, s_ref, out_ref, proj_ref, acc_ref):
    rows, width = proj_ref.shape
    half = width // 2
    proj_ref[:, pl.ds(0, half)] = jnp.dot(rows_ref[...], unit_ref[...], preferred_element_type=F32)
    proj_ref[:, pl.ds(half, half)] = jnp.dot(rows_ref[...], more_ref[...], preferred_element_type=F32)
    acc_ref[...] = jnp.zeros_like(acc_ref)

    def fold(v):
        return jnp.sum(v.reshape(TILE // 8, 8, width), axis=0)

    @pl.loop(0, rows // TILE)
    def _(i):
        at = pl.ds(pl.multiple_of(i * TILE, TILE), TILE)
        c1, s1 = base_angle(proj_ref[at, :])
        c_ref[at, :] = c1
        s_ref[at, :] = s1
        two = c1 + c1
        acc_ref[0] += fold(c1)
        acc_ref[KNOTS - 1] += fold(s1)
        cp, sp, cc, sc = jnp.ones_like(c1), jnp.zeros_like(c1), c1, s1
        for k in range(1, KNOTS - 1):
            cp, cc = cc, two * cc - cp
            sp, sc = sc, two * sc - sp
            acc_ref[k] += fold(cc)
            acc_ref[KNOTS - 1 + k] += fold(sc)

    out_ref[...] = jnp.sum(acc_ref[...], axis=1)
    for k in range(1, KNOTS):
        out_ref[pl.ds(k - 1, 1), :] -= rows * TARGET[k]


def grad_kernel(total_rows, steps, along_x, c_ref, s_ref, sums_ref, unit_ref, more_ref, *refs):
    out_refs, (g_ref, rep_ref) = refs[:-2], refs[-2:]
    rows, width = g_ref.shape
    block = rows // len(steps)
    here = lax.axis_index("x")
    sums = jnp.sum(sums_ref[...], axis=0)
    for k in range(KNOTS):
        if k == 0:
            cos_off = jnp.full((1, width), total_rows * (1.0 - TARGET[0]), F32)
            sin_total = jnp.zeros((1, width), F32)
        else:
            cos_off = sums[k - 1 : k]
            sin_total = sums[KNOTS + k - 2 : KNOTS + k - 1]
        cos_coef = 2.0 * WEIGHT[k] * (cos_off / total_rows)
        sin_coef = 2.0 * WEIGHT[k] * (sin_total / total_rows)
        rep_ref[k] = jnp.broadcast_to(KNOT[k] * sin_coef, (8, width))
        rep_ref[KNOTS + k] = jnp.broadcast_to(-KNOT[k] * cos_coef, (8, width))

    def tile(i, chip):
        at = pl.ds(pl.multiple_of((i * along_x + chip) * TILE, TILE), TILE)
        c1 = c_ref[at, :].reshape(TILE // 8, 8, width)
        s1 = s_ref[at, :].reshape(TILE // 8, 8, width)
        two = c1 + c1
        a2 = jnp.zeros_like(c1)
        b2 = a2
        a1 = rep_ref[KNOTS - 1] + a2
        b1 = rep_ref[2 * KNOTS - 1] + a2
        for k in range(KNOTS - 2, 0, -1):
            a1, a2 = rep_ref[k] + (two * a1 - a2), a1
            b1, b2 = rep_ref[KNOTS + k] + (two * b1 - b2), b1
        g = rep_ref[0] + (c1 * a1 - a2) + s1 * b1
        return g.reshape(TILE, width).astype(BF16)

    for j, by in enumerate(steps):

        @pl.loop(0, block // TILE)
        def _(i):
            at = pl.ds(pl.multiple_of(j * block + i * TILE, TILE), TILE)
            g_ref[at, :] = tile(i, lax.rem(here + by, along_x))

    step, half = 512, width // 2
    for i in range(unit_ref.shape[0] // step):
        at = pl.ds(i * step, step)
        out = times_transposed(g_ref[:, pl.ds(0, half)], unit_ref[at, :]) + times_transposed(
            g_ref[:, pl.ds(half, half)], more_ref[at, :]
        )
        for j, out_ref in enumerate(out_refs):
            out_ref[:, at] = out[j * block : (j + 1) * block]


def times_transposed(a, b):
    return lax.dot_general(a, b, (((1,), (1,)), ((), ())), preferred_element_type=F32)


def call(kernel, outs, scratch, flops, moved, operands):
    whole = pl.BlockSpec(memory_space=pltpu.VMEM)
    return pl.pallas_call(
        kernel,
        out_shape=outs,
        in_specs=[whole] * operands,
        out_specs=jax.tree.map(lambda _: whole, outs),
        scratch_shapes=scratch,
        compiler_params=pltpu.CompilerParams(vmem_limit_bytes=16 << 20),
        cost_estimate=pl.CostEstimate(flops=flops, bytes_accessed=moved, transcendentals=0),
    )


def to_all(x, axes, peers):
    return lax.all_to_all(jnp.broadcast_to(x[None], (peers,) + x.shape), axes, 0, 0, tiled=True)


def turn(x, axis, by):
    n = lax.axis_size(axis)
    return lax.ppermute(x, axis, [(i, (i + by) % n) for i in range(n)])


def local(embeddings, directions):
    zh, zl, along_x = lax.axis_size("zh"), lax.axis_size("zl"), lax.axis_size("x")
    batch = lax.axis_size("y")
    depth, width = directions.shape
    block = embeddings.shape[0] * zh * zl
    rows = block * along_x
    total_rows = float(2 * rows * batch)
    sds = jax.ShapeDtypeStruct

    theirs = turn(directions, "c", 1)
    units = [
        call(unit_kernel, sds((depth, width), BF16), (), 4 * depth * width, 4 * depth * width, 1)(columns)
        for columns in (directions, theirs)
    ]
    held = to_all(embeddings, "zh", zh).reshape(-1, depth)
    held = to_all(held, ("zl", "x"), zl * along_x).reshape(rows, depth)

    c1, s1, sums = call(
        sums_kernel,
        (sds((rows, 2 * width), F32), sds((rows, 2 * width), F32), sds((2 * KNOTS - 2, 2 * width), F32)),
        (pltpu.VMEM((rows, 2 * width), F32), pltpu.VMEM((2 * KNOTS - 2, 8, 2 * width), F32)),
        4 * rows * depth * width,
        8 * rows * depth,
        3,
    )(held, *units)
    swapped = turn(sums, "c", 1)
    sums = sums + jnp.concatenate([swapped[:, width:], swapped[:, :width]], axis=1)
    sums = to_all(sums.astype(LINK), "y", batch).astype(F32)

    def grad(steps):
        outs = call(
            functools.partial(grad_kernel, total_rows, steps, along_x),
            [sds((block, depth), F32)] * len(steps),
            (pltpu.VMEM((len(steps) * block, 2 * width), BF16), pltpu.VMEM((2 * KNOTS, 8, 2 * width), F32)),
            4 * len(steps) * block * depth * width,
            4 * len(steps) * block * depth,
            5,
        )(c1, s1, sums, *units)
        return dict(zip(steps, outs))

    parts = grad((2, 1, along_x - 1, 0))
    for by in (2, 1, along_x - 1):
        parts[by] = turn(parts[by].astype(LINK), "x", by)
    part = sum(p.astype(F32) for p in parts.values()).astype(LINK)
    part = lax.all_to_all(part.reshape(zl * zh, -1, depth), ("zl", "zh"), 0, 0, tiled=True)
    return jnp.sum(part.astype(F32), axis=0)


def solution(mesh):
    fine = Mesh(mesh.devices.reshape(8, 4, 3, 4, 2), ("y", "zh", "zl", "x", "c"))
    along = ("zh", "zl", "x", "c")
    rows = P(("y",) + along, None)

    return jax.shard_map(local, mesh=fine, in_specs=(rows, P(None, along)), out_specs=rows, check_vma=False)
```

```python
import functools
import math

import jax
import jax.numpy as jnp
from jax import lax
from jax.experimental import pallas as pl
from jax.experimental.pallas import tpu as pltpu
from jax.sharding import Mesh, PartitionSpec as P


KNOTS = 17
STEP = 3.0 / (KNOTS - 1)
KNOT = [k * STEP for k in range(KNOTS)]
TARGET = [math.exp(-0.5 * t * t) for t in KNOT]
WEIGHT = [(0.5 if k in (0, KNOTS - 1) else 1.0) * STEP * TARGET[k] for k in range(KNOTS)]
TURN = (6.28125, 0.0019340515136719, 1.2556659146e-06)
TILE = 16
F32 = jnp.float32
BF16 = jnp.bfloat16
LINK = jnp.float16


def base_angle(proj):
    theta = proj * STEP
    turns = jnp.round(theta * (0.5 / math.pi))
    q = 0.25 * (((theta - turns * TURN[0]) - turns * TURN[1]) - turns * TURN[2])
    z = q * q
    s = q * (1.0 + z * (-1.0 / 6 + z * (1.0 / 120 + z * (-1.0 / 5040 + z * (1.0 / 362880)))))
    c = 1.0 - z * (0.5 + z * (-1.0 / 24 + z * (1.0 / 720 + z * (-1.0 / 40320))))
    s2 = 2.0 * s * c
    c2 = 1.0 - 2.0 * s * s
    return 1.0 - 2.0 * s2 * s2, 2.0 * s2 * c2


def unit_kernel(dir_ref, unit_ref):
    width = dir_ref.shape[1]
    rows = 256
    total = jnp.zeros((8, width), F32)
    for i in range(dir_ref.shape[0] // rows):
        w = dir_ref[pl.ds(i * rows, rows), :].astype(F32)
        total = total + jnp.sum((w * w).reshape(rows // 8, 8, width), axis=0)
    inv = 1.0 / jnp.sqrt(jnp.sum(total, axis=0, keepdims=True) + 1e-06)
    for i in range(dir_ref.shape[0] // rows):
        w = dir_ref[pl.ds(i * rows, rows), :].astype(F32)
        unit_ref[pl.ds(i * rows, rows), :] = (w * inv).astype(BF16)


def sums_kernel(rows_ref, unit_ref, c_ref, s_ref, out_ref, proj_ref, acc_ref):
    rows, width = proj_ref.shape
    tile = 2 * TILE
    proj_ref[...] = jnp.dot(rows_ref[...], unit_ref[...], preferred_element_type=F32)
    acc_ref[...] = jnp.zeros_like(acc_ref)

    def fold(v):
        return jnp.sum(v.reshape(tile // 8, 8, width), axis=0)

    @pl.loop(0, rows // tile)
    def _(i):
        at = pl.ds(pl.multiple_of(i * tile, tile), tile)
        c1, s1 = base_angle(proj_ref[at, :])
        c_ref[at, :] = c1
        s_ref[at, :] = s1
        two = c1 + c1
        acc_ref[0] += fold(c1)
        acc_ref[KNOTS - 1] += fold(s1)
        cp, sp, cc, sc = jnp.ones_like(c1), jnp.zeros_like(c1), c1, s1
        for k in range(1, KNOTS - 1):
            cp, cc = cc, two * cc - cp
            sp, sc = sc, two * sc - sp
            acc_ref[k] += fold(cc)
            acc_ref[KNOTS - 1 + k] += fold(sc)

    out_ref[...] = jnp.sum(acc_ref[...], axis=1)
    for k in range(1, KNOTS):
        out_ref[pl.ds(k - 1, 1), :] -= rows * TARGET[k]


def grad_kernel(total_rows, steps, along_x, c_ref, s_ref, c2_ref, s2_ref, sums_ref, sums2_ref, unit_ref, more_ref, *refs):
    out_refs, (g_ref, rep_ref) = refs[:-2], refs[-2:]
    rows, width = g_ref.shape
    block = rows // len(steps)
    here = lax.axis_index("x")
    sums = jnp.concatenate([sums_ref[...], sums2_ref[...]], axis=1)
    for k in range(KNOTS):
        if k == 0:
            cos_off = jnp.full((1, width), total_rows * (1.0 - TARGET[0]), F32)
            sin_total = jnp.zeros((1, width), F32)
        else:
            cos_off = sums[k - 1 : k]
            sin_total = sums[KNOTS + k - 2 : KNOTS + k - 1]
        cos_coef = 2.0 * WEIGHT[k] * (cos_off / total_rows)
        sin_coef = 2.0 * WEIGHT[k] * (sin_total / total_rows)
        rep_ref[k] = jnp.broadcast_to(KNOT[k] * sin_coef, (8, width))
        rep_ref[KNOTS + k] = jnp.broadcast_to(-KNOT[k] * cos_coef, (8, width))

    def tile(i, chip):
        at = pl.ds(pl.multiple_of((i * along_x + chip) * TILE, TILE), TILE)
        c1 = jnp.concatenate([c_ref[at, :], c2_ref[at, :]], axis=1).reshape(TILE // 8, 8, width)
        s1 = jnp.concatenate([s_ref[at, :], s2_ref[at, :]], axis=1).reshape(TILE // 8, 8, width)
        two = c1 + c1
        a2 = jnp.zeros_like(c1)
        b2 = a2
        a1 = rep_ref[KNOTS - 1] + a2
        b1 = rep_ref[2 * KNOTS - 1] + a2
        for k in range(KNOTS - 2, 0, -1):
            a1, a2 = rep_ref[k] + (two * a1 - a2), a1
            b1, b2 = rep_ref[KNOTS + k] + (two * b1 - b2), b1
        g = rep_ref[0] + (c1 * a1 - a2) + s1 * b1
        return g.reshape(TILE, width).astype(BF16)

    for j, by in enumerate(steps):

        @pl.loop(0, block // TILE)
        def _(i):
            at = pl.ds(pl.multiple_of(j * block + i * TILE, TILE), TILE)
            g_ref[at, :] = tile(i, lax.rem(here + by, along_x))

    step, half = 512, width // 2
    for i in range(unit_ref.shape[0] // step):
        at = pl.ds(i * step, step)
        out = times_transposed(g_ref[:, pl.ds(0, half)], unit_ref[at, :]) + times_transposed(
            g_ref[:, pl.ds(half, half)], more_ref[at, :]
        )
        for j, out_ref in enumerate(out_refs):
            out_ref[:, at] = out[j * block : (j + 1) * block]


def times_transposed(a, b):
    return lax.dot_general(a, b, (((1,), (1,)), ((), ())), preferred_element_type=F32)


def call(kernel, outs, scratch, flops, moved, operands):
    whole = pl.BlockSpec(memory_space=pltpu.VMEM)
    return pl.pallas_call(
        kernel,
        out_shape=outs,
        in_specs=[whole] * operands,
        out_specs=jax.tree.map(lambda _: whole, outs),
        scratch_shapes=scratch,
        compiler_params=pltpu.CompilerParams(vmem_limit_bytes=16 << 20),
        cost_estimate=pl.CostEstimate(flops=flops, bytes_accessed=moved, transcendentals=0),
    )


def to_all(x, axes, peers):
    return lax.all_to_all(jnp.broadcast_to(x[None], (peers,) + x.shape), axes, 0, 0, tiled=True)


def turn(x, axis, by):
    n = lax.axis_size(axis)
    return lax.ppermute(x, axis, [(i, (i + by) % n) for i in range(n)])


def local(embeddings, directions):
    zh, zl, along_x = lax.axis_size("zh"), lax.axis_size("zl"), lax.axis_size("x")
    batch = lax.axis_size("y")
    depth, width = directions.shape
    block = embeddings.shape[0] * zh * zl
    rows = block * along_x
    total_rows = float(2 * rows * batch)
    sds = jax.ShapeDtypeStruct

    held = to_all(embeddings, "zh", zh).reshape(-1, depth)
    theirs = turn(directions, "c", 1)
    units = []
    for columns in (directions, theirs):
        units.append(call(unit_kernel, sds((depth, width), BF16), (), 4 * depth * width, 4 * depth * width, 1)(columns))
    held, units = lax.optimization_barrier((held, units))
    held = to_all(held, ("zl", "x"), zl * along_x).reshape(rows, depth)

    def sums_of(unit):
        return call(
            sums_kernel,
            (sds((rows, width), F32), sds((rows, width), F32), sds((2 * KNOTS - 2, width), F32)),
            (pltpu.VMEM((rows, width), F32), pltpu.VMEM((2 * KNOTS - 2, 8, width), F32)),
            2 * rows * depth * width,
            4 * rows * depth,
            2,
        )(held, unit)

    c2, s2, sums = sums_of(units[1])
    arrived = turn(sums, "c", 1)
    c1, s1, sums = sums_of(units[0])
    sums = to_all((sums + arrived).astype(LINK), "y", batch)
    sums = jnp.sum(sums.astype(F32), axis=0)
    sums2 = turn(sums, "c", 1)

    def grad(steps):
        outs = call(
            functools.partial(grad_kernel, total_rows, steps, along_x),
            [sds((block, depth), F32)] * len(steps),
            (pltpu.VMEM((len(steps) * block, 2 * width), BF16), pltpu.VMEM((2 * KNOTS, 8, 2 * width), F32)),
            4 * len(steps) * block * depth * width,
            4 * len(steps) * block * depth,
            8,
        )(c1, s1, c2, s2, sums, sums2, *units)
        return dict(zip(steps, outs))

    parts = grad((2, 1, along_x - 1, 0))
    for by in (2, 1, along_x - 1):
        parts[by] = turn(parts[by].astype(LINK), "x", by)
    part = sum(p.astype(F32) for p in parts.values()).astype(LINK)
    part = lax.all_to_all(part.reshape(zl * zh, -1, depth), ("zl", "zh"), 0, 0, tiled=True)
    return jnp.sum(part.astype(F32), axis=0)


def solution(mesh):
    fine = Mesh(mesh.devices.reshape(8, 4, 3, 4, 2), ("y", "zh", "zl", "x", "c"))
    along = ("zh", "zl", "x", "c")
    rows = P(("y",) + along, None)

    return jax.shard_map(local, mesh=fine, in_specs=(rows, P(None, along)), out_specs=rows, check_vma=False)
```

```python
import functools
import math

import jax
import jax.numpy as jnp
from jax import lax
from jax.experimental import pallas as pl
from jax.experimental.pallas import tpu as pltpu
from jax.sharding import Mesh, PartitionSpec as P


KNOTS = 17
STEP = 3.0 / (KNOTS - 1)
KNOT = [k * STEP for k in range(KNOTS)]
TARGET = [math.exp(-0.5 * t * t) for t in KNOT]
WEIGHT = [(0.5 if k in (0, KNOTS - 1) else 1.0) * STEP * TARGET[k] for k in range(KNOTS)]
TURN = (6.28125, 0.0019340515136719, 1.2556659146e-06)
TILE = 16
F32 = jnp.float32
BF16 = jnp.bfloat16
LINK = jnp.float16


def base_angle(proj):
    theta = proj * STEP
    turns = jnp.round(theta * (0.5 / math.pi))
    q = 0.25 * (((theta - turns * TURN[0]) - turns * TURN[1]) - turns * TURN[2])
    z = q * q
    s = q * (1.0 + z * (-1.0 / 6 + z * (1.0 / 120 + z * (-1.0 / 5040 + z * (1.0 / 362880)))))
    c = 1.0 - z * (0.5 + z * (-1.0 / 24 + z * (1.0 / 720 + z * (-1.0 / 40320))))
    s2 = 2.0 * s * c
    c2 = 1.0 - 2.0 * s * s
    return 1.0 - 2.0 * s2 * s2, 2.0 * s2 * c2


def unit_kernel(dir_ref, unit_ref):
    width = dir_ref.shape[1]
    rows = 256
    total = jnp.zeros((8, width), F32)
    for i in range(dir_ref.shape[0] // rows):
        w = dir_ref[pl.ds(i * rows, rows), :].astype(F32)
        total = total + jnp.sum((w * w).reshape(rows // 8, 8, width), axis=0)
    inv = 1.0 / jnp.sqrt(jnp.sum(total, axis=0, keepdims=True) + 1e-06)
    for i in range(dir_ref.shape[0] // rows):
        w = dir_ref[pl.ds(i * rows, rows), :].astype(F32)
        unit_ref[pl.ds(i * rows, rows), :] = (w * inv).astype(BF16)


def sums_kernel(rows_ref, unit_ref, c_ref, s_ref, out_ref, proj_ref, acc_ref):
    rows, width = proj_ref.shape
    tile = 2 * TILE
    proj_ref[...] = jnp.dot(rows_ref[...], unit_ref[...], preferred_element_type=F32)
    acc_ref[...] = jnp.zeros_like(acc_ref)

    def fold(v):
        return jnp.sum(v.reshape(tile // 8, 8, width), axis=0)

    @pl.loop(0, rows // tile)
    def _(i):
        at = pl.ds(pl.multiple_of(i * tile, tile), tile)
        c1, s1 = base_angle(proj_ref[at, :])
        c_ref[at, :] = c1
        s_ref[at, :] = s1
        two = c1 + c1
        acc_ref[0] += fold(c1)
        acc_ref[KNOTS - 1] += fold(s1)
        cp, sp, cc, sc = jnp.ones_like(c1), jnp.zeros_like(c1), c1, s1
        for k in range(1, KNOTS - 1):
            cp, cc = cc, two * cc - cp
            sp, sc = sc, two * sc - sp
            acc_ref[k] += fold(cc)
            acc_ref[KNOTS - 1 + k] += fold(sc)

    out_ref[...] = jnp.sum(acc_ref[...], axis=1)
    for k in range(1, KNOTS):
        out_ref[pl.ds(k - 1, 1), :] -= rows * TARGET[k]


def grad_kernel(total_rows, steps, along_x, c_ref, s_ref, c2_ref, s2_ref, sums_ref, unit_ref, more_ref, *refs):
    out_refs, (g_ref, rep_ref) = refs[:-2], refs[-2:]
    rows, width = g_ref.shape
    block = rows // len(steps)
    here = lax.axis_index("x")
    core = lax.axis_index("c")
    sums = [jnp.sum(sums_ref[:, pl.ds(i, 1)], axis=(0, 1)) for i in (core, 1 - core)]
    sums = jnp.concatenate(sums, axis=1)
    for k in range(KNOTS):
        if k == 0:
            cos_off = jnp.full((1, width), total_rows * (1.0 - TARGET[0]), F32)
            sin_total = jnp.zeros((1, width), F32)
        else:
            cos_off = sums[k - 1 : k]
            sin_total = sums[KNOTS + k - 2 : KNOTS + k - 1]
        cos_coef = 2.0 * WEIGHT[k] * (cos_off / total_rows)
        sin_coef = 2.0 * WEIGHT[k] * (sin_total / total_rows)
        rep_ref[k] = jnp.broadcast_to(KNOT[k] * sin_coef, (8, width))
        rep_ref[KNOTS + k] = jnp.broadcast_to(-KNOT[k] * cos_coef, (8, width))

    def tile(i, chip):
        at = pl.ds(pl.multiple_of((i * along_x + chip) * TILE, TILE), TILE)
        c1 = jnp.concatenate([c_ref[at, :], c2_ref[at, :]], axis=1).reshape(TILE // 8, 8, width)
        s1 = jnp.concatenate([s_ref[at, :], s2_ref[at, :]], axis=1).reshape(TILE // 8, 8, width)
        two = c1 + c1
        a2 = jnp.zeros_like(c1)
        b2 = a2
        a1 = rep_ref[KNOTS - 1] + a2
        b1 = rep_ref[2 * KNOTS - 1] + a2
        for k in range(KNOTS - 2, 0, -1):
            a1, a2 = rep_ref[k] + (two * a1 - a2), a1
            b1, b2 = rep_ref[KNOTS + k] + (two * b1 - b2), b1
        g = rep_ref[0] + (c1 * a1 - a2) + s1 * b1
        return g.reshape(TILE, width).astype(BF16)

    for j, by in enumerate(steps):

        @pl.loop(0, block // TILE)
        def _(i):
            at = pl.ds(pl.multiple_of(j * block + i * TILE, TILE), TILE)
            g_ref[at, :] = tile(i, lax.rem(here + by, along_x))

    step, half = 512, width // 2
    for i in range(unit_ref.shape[0] // step):
        at = pl.ds(i * step, step)
        out = times_transposed(g_ref[:, pl.ds(0, half)], unit_ref[at, :]) + times_transposed(
            g_ref[:, pl.ds(half, half)], more_ref[at, :]
        )
        for j, out_ref in enumerate(out_refs):
            out_ref[:, at] = out[j * block : (j + 1) * block]


def times_transposed(a, b):
    return lax.dot_general(a, b, (((1,), (1,)), ((), ())), preferred_element_type=F32)


def call(kernel, outs, scratch, flops, moved, operands):
    whole = pl.BlockSpec(memory_space=pltpu.VMEM)
    return pl.pallas_call(
        kernel,
        out_shape=outs,
        in_specs=[whole] * operands,
        out_specs=jax.tree.map(lambda _: whole, outs),
        scratch_shapes=scratch,
        compiler_params=pltpu.CompilerParams(vmem_limit_bytes=16 << 20),
        cost_estimate=pl.CostEstimate(flops=flops, bytes_accessed=moved, transcendentals=0),
    )


def to_all(x, axes, peers):
    return lax.all_to_all(jnp.broadcast_to(x[None], (peers,) + x.shape), axes, 0, 0, tiled=True)


def turn(x, axis, by):
    n = lax.axis_size(axis)
    return lax.ppermute(x, axis, [(i, (i + by) % n) for i in range(n)])


def local(embeddings, directions):
    zh, zl, along_x = lax.axis_size("zh"), lax.axis_size("zl"), lax.axis_size("x")
    batch = lax.axis_size("y")
    depth, width = directions.shape
    block = embeddings.shape[0] * zh * zl
    rows = block * along_x
    total_rows = float(2 * rows * batch)
    sds = jax.ShapeDtypeStruct

    held = to_all(embeddings, "zh", zh).reshape(-1, depth)
    theirs = turn(directions, "c", 1)
    units = []
    for columns in (directions, theirs):
        units.append(call(unit_kernel, sds((depth, width), BF16), (), 4 * depth * width, 4 * depth * width, 1)(columns))
    held = to_all(held, ("zl", "x"), zl * along_x).reshape(rows, depth)

    def sums_of(unit):
        return call(
            sums_kernel,
            (sds((rows, width), F32), sds((rows, width), F32), sds((2 * KNOTS - 2, width), F32)),
            (pltpu.VMEM((rows, width), F32), pltpu.VMEM((2 * KNOTS - 2, 8, width), F32)),
            2 * rows * depth * width,
            4 * rows * depth,
            2,
        )(held, unit)

    c2, s2, sums = sums_of(units[1])
    arrived = turn(sums, "c", 1)
    c1, s1, sums = sums_of(units[0])
    sums = to_all((sums + arrived).astype(LINK), ("y", "c"), 2 * batch).astype(F32)
    sums = sums.reshape(batch, 2, 2 * KNOTS - 2, width)

    def grad(steps):
        outs = call(
            functools.partial(grad_kernel, total_rows, steps, along_x),
            [sds((block, depth), F32)] * len(steps),
            (pltpu.VMEM((len(steps) * block, 2 * width), BF16), pltpu.VMEM((2 * KNOTS, 8, 2 * width), F32)),
            4 * len(steps) * block * depth * width,
            4 * len(steps) * block * depth,
            7,
        )(c1, s1, c2, s2, sums, *units)
        return dict(zip(steps, outs))

    parts = grad((2, 1, along_x - 1, 0))
    for by in (2, 1, along_x - 1):
        parts[by] = turn(parts[by].astype(LINK), "x", by)
    part = sum(p.astype(F32) for p in parts.values()).astype(LINK)
    part = lax.all_to_all(part.reshape(zl * zh, -1, depth), ("zl", "zh"), 0, 0, tiled=True)
    return jnp.sum(part.astype(F32), axis=0)


def solution(mesh):
    fine = Mesh(mesh.devices.reshape(8, 4, 3, 4, 2), ("y", "zh", "zl", "x", "c"))
    along = ("zh", "zl", "x", "c")
    rows = P(("y",) + along, None)

    return jax.shard_map(local, mesh=fine, in_specs=(rows, P(None, along)), out_specs=rows, check_vma=False)
```

```python
import functools
import math

import jax
import jax.numpy as jnp
from jax import lax
from jax.experimental import pallas as pl
from jax.experimental.pallas import tpu as pltpu
from jax.sharding import Mesh, PartitionSpec as P


KNOTS = 17
STEP = 3.0 / (KNOTS - 1)
KNOT = [k * STEP for k in range(KNOTS)]
TARGET = [math.exp(-0.5 * t * t) for t in KNOT]
WEIGHT = [(0.5 if k in (0, KNOTS - 1) else 1.0) * STEP * TARGET[k] for k in range(KNOTS)]
TURN = (6.28125, 0.0019340515136719, 1.2556659146e-06)
TILE = 16
F32 = jnp.float32
BF16 = jnp.bfloat16
LINK = jnp.float16


def base_angle(proj):
    theta = proj * STEP
    turns = jnp.round(theta * (0.5 / math.pi))
    q = 0.25 * (((theta - turns * TURN[0]) - turns * TURN[1]) - turns * TURN[2])
    z = q * q
    s = q * (1.0 + z * (-1.0 / 6 + z * (1.0 / 120 + z * (-1.0 / 5040 + z * (1.0 / 362880)))))
    c = 1.0 - z * (0.5 + z * (-1.0 / 24 + z * (1.0 / 720 + z * (-1.0 / 40320))))
    s2 = 2.0 * s * c
    c2 = 1.0 - 2.0 * s * s
    return 1.0 - 2.0 * s2 * s2, 2.0 * s2 * c2


def unit_kernel(dir_ref, unit_ref):
    width = dir_ref.shape[1]
    rows = 256
    total = jnp.zeros((8, width), F32)
    for i in range(dir_ref.shape[0] // rows):
        w = dir_ref[pl.ds(i * rows, rows), :].astype(F32)
        total = total + jnp.sum((w * w).reshape(rows // 8, 8, width), axis=0)
    inv = 1.0 / jnp.sqrt(jnp.sum(total, axis=0, keepdims=True) + 1e-06)
    for i in range(dir_ref.shape[0] // rows):
        w = dir_ref[pl.ds(i * rows, rows), :].astype(F32)
        unit_ref[pl.ds(i * rows, rows), :] = (w * inv).astype(BF16)


def sums_kernel(rows_ref, unit_ref, more_ref, c_ref, s_ref, out_ref, proj_ref, acc_ref):
    rows, width = proj_ref.shape
    half = width // 2
    proj_ref[:, pl.ds(0, half)] = jnp.dot(rows_ref[...], unit_ref[...], preferred_element_type=F32)
    proj_ref[:, pl.ds(half, half)] = jnp.dot(rows_ref[...], more_ref[...], preferred_element_type=F32)
    acc_ref[...] = jnp.zeros_like(acc_ref)

    def fold(v):
        return jnp.sum(v.reshape(TILE // 8, 8, width), axis=0)

    @pl.loop(0, rows // TILE)
    def _(i):
        at = pl.ds(pl.multiple_of(i * TILE, TILE), TILE)
        c1, s1 = base_angle(proj_ref[at, :])
        c_ref[at, :] = c1
        s_ref[at, :] = s1
        two = c1 + c1
        acc_ref[0] += fold(c1)
        acc_ref[KNOTS - 1] += fold(s1)
        cp, sp, cc, sc = jnp.ones_like(c1), jnp.zeros_like(c1), c1, s1
        for k in range(1, KNOTS - 1):
            cp, cc = cc, two * cc - cp
            sp, sc = sc, two * sc - sp
            acc_ref[k] += fold(cc)
            acc_ref[KNOTS - 1 + k] += fold(sc)

    out_ref[...] = jnp.sum(acc_ref[...], axis=1)
    for k in range(1, KNOTS):
        out_ref[pl.ds(k - 1, 1), :] -= rows * TARGET[k]


def grad_kernel(total_rows, steps, along_x, c_ref, s_ref, sums_ref, unit_ref, more_ref, *refs):
    out_refs, (g_ref, rep_ref) = refs[:-2], refs[-2:]
    rows, width = g_ref.shape
    block = rows // len(steps)
    sums = jnp.sum(sums_ref[...], axis=0)
    for k in range(KNOTS):
        if k == 0:
            cos_off = jnp.full((1, width), total_rows * (1.0 - TARGET[0]), F32)
            sin_total = jnp.zeros((1, width), F32)
        else:
            cos_off = sums[k - 1 : k]
            sin_total = sums[KNOTS + k - 2 : KNOTS + k - 1]
        cos_coef = 2.0 * WEIGHT[k] * (cos_off / total_rows)
        sin_coef = 2.0 * WEIGHT[k] * (sin_total / total_rows)
        rep_ref[k] = jnp.broadcast_to(KNOT[k] * sin_coef, (8, width))
        rep_ref[KNOTS + k] = jnp.broadcast_to(-KNOT[k] * cos_coef, (8, width))

    def tile(i, chip):
        at = pl.ds(pl.multiple_of((i * along_x + chip) * TILE, TILE), TILE)
        c1 = c_ref[at, :].reshape(TILE // 8, 8, width)
        s1 = s_ref[at, :].reshape(TILE // 8, 8, width)
        two = c1 + c1
        a2 = jnp.zeros_like(c1)
        b2 = a2
        a1 = rep_ref[KNOTS - 1] + a2
        b1 = rep_ref[2 * KNOTS - 1] + a2
        for k in range(KNOTS - 2, 0, -1):
            a1, a2 = rep_ref[k] + (two * a1 - a2), a1
            b1, b2 = rep_ref[KNOTS + k] + (two * b1 - b2), b1
        g = rep_ref[0] + (c1 * a1 - a2) + s1 * b1
        return g.reshape(TILE, width).astype(BF16)

    for j, by in enumerate(steps):

        @pl.loop(0, block // TILE)
        def _(i):
            at = pl.ds(pl.multiple_of(j * block + i * TILE, TILE), TILE)
            g_ref[at, :] = tile(i, by)

    step, half = 512, width // 2
    for i in range(unit_ref.shape[0] // step):
        at = pl.ds(i * step, step)
        out = times_transposed(g_ref[:, pl.ds(0, half)], unit_ref[at, :]) + times_transposed(
            g_ref[:, pl.ds(half, half)], more_ref[at, :]
        )
        out_refs[0][:, at] = out


def times_transposed(a, b):
    return lax.dot_general(a, b, (((1,), (1,)), ((), ())), preferred_element_type=F32)


def call(kernel, outs, scratch, flops, moved, operands):
    whole = pl.BlockSpec(memory_space=pltpu.VMEM)
    return pl.pallas_call(
        kernel,
        out_shape=outs,
        in_specs=[whole] * operands,
        out_specs=jax.tree.map(lambda _: whole, outs),
        scratch_shapes=scratch,
        compiler_params=pltpu.CompilerParams(vmem_limit_bytes=16 << 20),
        cost_estimate=pl.CostEstimate(flops=flops, bytes_accessed=moved, transcendentals=0),
    )


def to_all(x, axes, peers):
    return lax.all_to_all(jnp.broadcast_to(x[None], (peers,) + x.shape), axes, 0, 0, tiled=True)


def turn(x, axis, by):
    n = lax.axis_size(axis)
    return lax.ppermute(x, axis, [(i, (i + by) % n) for i in range(n)])


def local(embeddings, directions):
    zh, zl, along_x = lax.axis_size("zh"), lax.axis_size("zl"), lax.axis_size("x")
    batch = lax.axis_size("y")
    depth, width = directions.shape
    block = embeddings.shape[0] * zh * zl
    rows = block * along_x
    total_rows = float(2 * rows * batch)
    sds = jax.ShapeDtypeStruct

    with jax.named_scope("columns"):
        theirs = turn(directions, "c", 1)
    units = [
        call(unit_kernel, sds((depth, width), BF16), (), 4 * depth * width, 4 * depth * width, 1)(columns)
        for columns in (directions, theirs)
    ]
    with jax.named_scope("far"):
        held = to_all(embeddings, "zh", zh).reshape(-1, depth)
    with jax.named_scope("near"):
        held = to_all(held, ("zl", "x"), zl * along_x).reshape(rows, depth)

    c1, s1, sums = call(
        sums_kernel,
        (sds((rows, 2 * width), F32), sds((rows, 2 * width), F32), sds((2 * KNOTS - 2, 2 * width), F32)),
        (pltpu.VMEM((rows, 2 * width), F32), pltpu.VMEM((2 * KNOTS - 2, 8, 2 * width), F32)),
        4 * rows * depth * width,
        8 * rows * depth,
        3,
    )(held, *units)
    swapped = turn(sums, "c", 1)
    sums = sums + jnp.concatenate([swapped[:, width:], swapped[:, :width]], axis=1)
    sums = to_all(sums.astype(LINK), "y", batch).astype(F32)

    part = call(
        functools.partial(grad_kernel, total_rows, tuple(range(along_x)), along_x),
        sds((rows, depth), F32),
        (pltpu.VMEM((rows, 2 * width), BF16), pltpu.VMEM((2 * KNOTS, 8, 2 * width), F32)),
        4 * rows * depth * width,
        4 * rows * depth,
        5,
    )(c1, s1, sums, *units)
    part = lax.all_to_all(part.astype(LINK).reshape(along_x, block, depth), "x", 0, 0, tiled=True)
    part = jnp.sum(part.astype(F32), axis=0).astype(LINK)
    part = lax.all_to_all(part.reshape(zl * zh, -1, depth), ("zl", "zh"), 0, 0, tiled=True)
    return jnp.sum(part.astype(F32), axis=0)


def solution(mesh):
    fine = Mesh(mesh.devices.reshape(8, 4, 3, 4, 2), ("y", "zh", "zl", "x", "c"))
    along = ("zh", "zl", "x", "c")
    rows = P(("y",) + along, None)

    return jax.shard_map(local, mesh=fine, in_specs=(rows, P(None, along)), out_specs=rows, check_vma=False)
```

```python
import functools
import math

import jax
import jax.numpy as jnp
from jax import lax
from jax.experimental import pallas as pl
from jax.experimental.pallas import tpu as pltpu
from jax.sharding import Mesh, PartitionSpec as P


KNOTS = 17
STEP = 3.0 / (KNOTS - 1)
KNOT = [k * STEP for k in range(KNOTS)]
TARGET = [math.exp(-0.5 * t * t) for t in KNOT]
WEIGHT = [(0.5 if k in (0, KNOTS - 1) else 1.0) * STEP * TARGET[k] for k in range(KNOTS)]
TURN = (6.28125, 0.0019340515136719, 1.2556659146e-06)
TILE = 16
F32 = jnp.float32
BF16 = jnp.bfloat16
LINK = jnp.float16


def base_angle(proj):
    theta = proj * STEP
    turns = jnp.round(theta * (0.5 / math.pi))
    q = 0.25 * (((theta - turns * TURN[0]) - turns * TURN[1]) - turns * TURN[2])
    z = q * q
    s = q * (1.0 + z * (-1.0 / 6 + z * (1.0 / 120 + z * (-1.0 / 5040 + z * (1.0 / 362880)))))
    c = 1.0 - z * (0.5 + z * (-1.0 / 24 + z * (1.0 / 720 + z * (-1.0 / 40320))))
    s2 = 2.0 * s * c
    c2 = 1.0 - 2.0 * s * s
    return 1.0 - 2.0 * s2 * s2, 2.0 * s2 * c2


def unit_kernel(dir_ref, unit_ref):
    width = dir_ref.shape[1]
    rows = 256
    total = jnp.zeros((8, width), F32)
    for i in range(dir_ref.shape[0] // rows):
        w = dir_ref[pl.ds(i * rows, rows), :].astype(F32)
        total = total + jnp.sum((w * w).reshape(rows // 8, 8, width), axis=0)
    inv = 1.0 / jnp.sqrt(jnp.sum(total, axis=0, keepdims=True) + 1e-06)
    for i in range(dir_ref.shape[0] // rows):
        w = dir_ref[pl.ds(i * rows, rows), :].astype(F32)
        unit_ref[pl.ds(i * rows, rows), :] = (w * inv).astype(BF16)


def sums_kernel(rows_ref, unit_ref, more_ref, c_ref, s_ref, out_ref, proj_ref, acc_ref):
    rows, width = proj_ref.shape
    half = width // 2
    proj_ref[:, pl.ds(0, half)] = jnp.dot(rows_ref[...], unit_ref[...], preferred_element_type=F32)
    proj_ref[:, pl.ds(half, half)] = jnp.dot(rows_ref[...], more_ref[...], preferred_element_type=F32)
    acc_ref[...] = jnp.zeros_like(acc_ref)

    def fold(v):
        return jnp.sum(v.reshape(TILE // 8, 8, width), axis=0)

    @pl.loop(0, rows // TILE)
    def _(i):
        at = pl.ds(pl.multiple_of(i * TILE, TILE), TILE)
        c1, s1 = base_angle(proj_ref[at, :])
        c_ref[at, :] = c1
        s_ref[at, :] = s1
        two = c1 + c1
        acc_ref[0] += fold(c1)
        acc_ref[KNOTS - 1] += fold(s1)
        cp, sp, cc, sc = jnp.ones_like(c1), jnp.zeros_like(c1), c1, s1
        for k in range(1, KNOTS - 1):
            cp, cc = cc, two * cc - cp
            sp, sc = sc, two * sc - sp
            acc_ref[k] += fold(cc)
            acc_ref[KNOTS - 1 + k] += fold(sc)

    out_ref[...] = jnp.sum(acc_ref[...], axis=1)
    for k in range(1, KNOTS):
        out_ref[pl.ds(k - 1, 1), :] -= rows * TARGET[k]


def grad_kernel(total_rows, c_ref, s_ref, sums_ref, unit_ref, more_ref, *refs):
    out_refs, (g_ref, rep_ref) = refs[:-2], refs[-2:]
    rows, width = g_ref.shape
    sums = jnp.sum(sums_ref[...], axis=0)
    for k in range(KNOTS):
        if k == 0:
            cos_off = jnp.full((1, width), total_rows * (1.0 - TARGET[0]), F32)
            sin_total = jnp.zeros((1, width), F32)
        else:
            cos_off = sums[k - 1 : k]
            sin_total = sums[KNOTS + k - 2 : KNOTS + k - 1]
        cos_coef = 2.0 * WEIGHT[k] * (cos_off / total_rows)
        sin_coef = 2.0 * WEIGHT[k] * (sin_total / total_rows)
        rep_ref[k] = jnp.broadcast_to(KNOT[k] * sin_coef, (8, width))
        rep_ref[KNOTS + k] = jnp.broadcast_to(-KNOT[k] * cos_coef, (8, width))

    def tile(i):
        at = pl.ds(pl.multiple_of(i * TILE, TILE), TILE)
        c1 = c_ref[at, :].reshape(TILE // 8, 8, width)
        s1 = s_ref[at, :].reshape(TILE // 8, 8, width)
        two = c1 + c1
        a2 = jnp.zeros_like(c1)
        b2 = a2
        a1 = rep_ref[KNOTS - 1] + a2
        b1 = rep_ref[2 * KNOTS - 1] + a2
        for k in range(KNOTS - 2, 0, -1):
            a1, a2 = rep_ref[k] + (two * a1 - a2), a1
            b1, b2 = rep_ref[KNOTS + k] + (two * b1 - b2), b1
        g = rep_ref[0] + (c1 * a1 - a2) + s1 * b1
        return g.reshape(TILE, width).astype(BF16)

    @pl.loop(0, rows // TILE)
    def _(i):
        g_ref[pl.ds(pl.multiple_of(i * TILE, TILE), TILE), :] = tile(i)

    step, half = 512, width // 2
    for i in range(unit_ref.shape[0] // step):
        at = pl.ds(i * step, step)
        out = times_transposed(g_ref[:, pl.ds(0, half)], unit_ref[at, :]) + times_transposed(
            g_ref[:, pl.ds(half, half)], more_ref[at, :]
        )
        out_refs[0][:, at] = out


def times_transposed(a, b):
    return lax.dot_general(a, b, (((1,), (1,)), ((), ())), preferred_element_type=F32)


def call(kernel, outs, scratch, flops, moved, operands):
    whole = pl.BlockSpec(memory_space=pltpu.VMEM)
    return pl.pallas_call(
        kernel,
        out_shape=outs,
        in_specs=[whole] * operands,
        out_specs=jax.tree.map(lambda _: whole, outs),
        scratch_shapes=scratch,
        compiler_params=pltpu.CompilerParams(vmem_limit_bytes=16 << 20),
        cost_estimate=pl.CostEstimate(flops=flops, bytes_accessed=moved, transcendentals=0),
    )


def to_all(x, axes, peers):
    return lax.all_to_all(jnp.broadcast_to(x[None], (peers,) + x.shape), axes, 0, 0, tiled=True)


def turn(x, axis, by):
    n = lax.axis_size(axis)
    return lax.ppermute(x, axis, [(i, (i + by) % n) for i in range(n)])


def local(embeddings, directions):
    zh, zl, along_x = lax.axis_size("zh"), lax.axis_size("zl"), lax.axis_size("x")
    batch = lax.axis_size("y")
    depth, width = directions.shape
    block = embeddings.shape[0] * zh * zl
    rows = block * along_x
    total_rows = float(2 * rows * batch)
    sds = jax.ShapeDtypeStruct

    with jax.named_scope("columns"):
        theirs = turn(directions, "c", 1)
    units = [
        call(unit_kernel, sds((depth, width), BF16), (), 4 * depth * width, 4 * depth * width, 1)(columns)
        for columns in (directions, theirs)
    ]
    with jax.named_scope("far"):
        held = to_all(embeddings, "zh", zh).reshape(-1, depth)
    with jax.named_scope("near"):
        held = to_all(held, ("zl", "x"), zl * along_x).reshape(rows, depth)

    c1, s1, sums = call(
        sums_kernel,
        (sds((rows, 2 * width), F32), sds((rows, 2 * width), F32), sds((2 * KNOTS - 2, 2 * width), F32)),
        (pltpu.VMEM((rows, 2 * width), F32), pltpu.VMEM((2 * KNOTS - 2, 8, 2 * width), F32)),
        4 * rows * depth * width,
        8 * rows * depth,
        3,
    )(held, *units)
    swapped = turn(sums, "c", 1)
    sums = sums + jnp.concatenate([swapped[:, width:], swapped[:, :width]], axis=1)
    sums = to_all(sums.astype(LINK), "y", batch).astype(F32)

    part = call(
        functools.partial(grad_kernel, total_rows),
        sds((rows, depth), F32),
        (pltpu.VMEM((rows, 2 * width), BF16), pltpu.VMEM((2 * KNOTS, 8, 2 * width), F32)),
        4 * rows * depth * width,
        4 * rows * depth,
        5,
    )(c1, s1, sums, *units)
    part = lax.all_to_all(part.astype(LINK).reshape(zl * along_x, -1, depth), ("zl", "x"), 0, 0, tiled=True)
    part = jnp.sum(part.astype(F32), axis=0).astype(LINK).reshape(zh, -1, depth)
    part = lax.all_to_all(part, "zh", 0, 0, tiled=True)
    return jnp.sum(part.astype(F32), axis=0)


def solution(mesh):
    fine = Mesh(mesh.devices.reshape(8, 4, 3, 4, 2), ("y", "zh", "zl", "x", "c"))
    along = ("zh", "zl", "x", "c")
    rows = P(("y",) + along, None)

    return jax.shard_map(local, mesh=fine, in_specs=(rows, P(None, along)), out_specs=rows, check_vma=False)
```
